32 devices in a mesh: gx: 8 (over y, x, core), gy: 4 (over z).
Axes of the slice: x: 2, y: 2, z: 4, core: 2. Of those that a mesh axis runs over, the one named last changes fastest.
Arguments:
- dual_ops: float32 [8, 4, 1536, 1536], P('gx', 'gy')
- loads: float32 [8, 4, 2, 384, 128], P('gx', 'gy'), may hold values from -16 to 16
- coarse_rhs: float32 [8, 4, 6, 128], P('gx', 'gy'), may hold values from -288 to 288
- coarse_modes: float32 [8, 4, 2, 2, 6, 384], P('gx', 'gy'), as said below
- free_mask: int32 [8, 4, 2, 384], P('gx', 'gy'), may hold values from 0 to 1
- face_match: int32 [8, 4, 2, 384], P('gx', 'gy'), may hold values from 0 to 383, each once within a row
- coarse_rows: float32 [8, 4, 3, 6, 192], P('gx', 'gy'), as said below
Outputs:
- multipliers: float32 [8, 4, 2, 384, 128], P('gx', 'gy')
- projected: float32 [8, 4, 2, 384, 128], P('gx', 'gy')
The draws below stay inside these ranges and needn't reach their ends.
Inputs may be any that keep to these rules, and one draw needn't show every extreme that they name: The draws of coarse_modes, free_mask and coarse_rows belong together. coarse_modes[a,b,0,1] is zero on the last grid column and coarse_modes[a,b,1,1] on the last grid row. With C the symmetric positive definite coarse matrix whose entries are the sums of free times products of the coarse-mode images of two modes over all east and south face multipliers (G^T G restricted to free multipliers, in the order (a, b, mode)), coarse_rows[a,b,0] are the rows of the inverse of C for the modes of (a,b), up to rounding; coarse_rows[a,b,1] equals coarse_rows[a,b+1,0] and coarse_rows[a,b,2] equals coarse_rows[a+1,b,0], zero where that neighbour does not exist.
All inputs are finite; a program needn't handle non-finite values.
Results may differ from the reference program's by a relative error of at most 0.00029.
Values sent between devices are 32-bit elements; how exact they have to be, the bound alone decides.
A program may use at most 64 MiB of HBM per device.

```python
import jax
import jax.numpy as jnp
from jax import lax

LM = 1536
LF = 384
ITERS = 3
NCASE = 128
SX = 8
SY = 4
NC = 192


def coarse_frame(key):
    base = jax.random.fold_in(key, 9173)
    key_dirs, key_plane, key_weight, key_mask, key_other = jax.random.split(base, 5)
    directions = jax.random.normal(key_dirs, (SX, SY, 2, LF, 3), jnp.float32)
    directions = directions / jnp.sqrt(jnp.sum(directions * directions, axis=-1, keepdims=True) + 1e-06)
    plane = jax.random.uniform(key_plane, (SX, SY, 2, LF, 2), jnp.float32, -0.5, 0.5)
    face_index = jnp.arange(2)[None, None, :, None]
    first = jnp.where(face_index == 0, 0.5, plane[..., 0])
    second = jnp.where(face_index == 0, plane[..., 0], 0.5)
    points = jnp.stack([first, second, plane[..., 1]], axis=-1)
    weights = jnp.exp(jax.random.uniform(key_weight, (SX, SY, 2, LF), jnp.float32, jnp.log(0.5), jnp.log(2.0)))
    other_weights = jnp.exp(jax.random.uniform(key_other, (SX, SY, 2, LF), jnp.float32, jnp.log(0.5), jnp.log(2.0)))

    def images_at(where, scale):
        rotation = jnp.cross(where, directions)
        return jnp.concatenate([directions, rotation], axis=-1) * scale[..., None]
    offsets = jnp.array([[1.0, 0.0, 0.0], [0.0, 1.0, 0.0]], jnp.float32)[None, None, :, None, :]
    own_images = images_at(points, weights)
    other_images = -images_at(points - offsets, other_weights)
    row_index = jnp.arange(SX)[:, None, None, None]
    col_index = jnp.arange(SY)[None, :, None, None]
    exists = jnp.where(face_index == 0, col_index < SY - 1, row_index < SX - 1)
    other_images = other_images * exists[..., None].astype(jnp.float32)
    modes = jnp.stack([own_images, other_images], axis=3)
    modes = jnp.transpose(modes, (0, 1, 2, 3, 5, 4))
    mask = (jax.random.randint(key_mask, (SX, SY, 2, LF), 0, 8) < 6).astype(jnp.int32)
    empty = jnp.zeros((SX, SY, 6, LF), jnp.float32)
    own_part = jnp.stack([modes[:, :, 0, 0], modes[:, :, 1, 0]], axis=3)
    east_part = jnp.stack([modes[:, :, 0, 1], empty], axis=3)
    south_part = jnp.stack([empty, modes[:, :, 1, 1]], axis=3)
    kernel = jnp.stack([own_part, east_part, south_part], axis=2)
    masked = kernel * mask[:, :, None, None, :, :].astype(jnp.float32)
    blocks = jnp.einsum('abrjfk,absifk->abrjsi', masked, kernel, precision=lax.Precision.HIGHEST)
    row_moves = [jnp.eye(SX, SX, 0), jnp.eye(SX, SX, 0), jnp.eye(SX, SX, 1)]
    col_moves = [jnp.eye(SY, SY, 0), jnp.eye(SY, SY, 1), jnp.eye(SY, SY, 0)]
    coarse = jnp.zeros((SX, SY, 6, SX, SY, 6), jnp.float32)
    for first_role in range(3):
        for second_role in range(3):
            coarse = coarse + jnp.einsum('abji,ac,bd,ae,bf->cdjefi', blocks[:, :, first_role, :, second_role, :], row_moves[first_role], col_moves[first_role], row_moves[second_role], col_moves[second_role], precision=lax.Precision.HIGHEST)
    coarse = coarse.reshape(NC, NC)
    inverse = jnp.linalg.inv(coarse)
    identity = jnp.eye(NC, dtype=jnp.float32)
    inverse = jnp.dot(inverse, 2.0 * identity - jnp.dot(coarse, inverse, precision=lax.Precision.HIGHEST), precision=lax.Precision.HIGHEST)
    inverse = 0.5 * (inverse + inverse.T)
    grid_rows = inverse.reshape(SX, SY, 6, NC)
    padded = jnp.pad(grid_rows, ((0, 1), (0, 1), (0, 0), (0, 0)))
    rows = jnp.stack([grid_rows, padded[:SX, 1:SY + 1], padded[1:SX + 1, :SY]], axis=2)
    return (modes, mask, rows)


def draw_coarse_modes(key, part):
    return coarse_frame(key)[0]


def draw_free_mask(key, part):
    return coarse_frame(key)[1]


def draw_coarse_rows(key, part):
    return coarse_frame(key)[2]


def draw_dual_ops(key, part):
    base = jax.random.fold_in(key, 31)
    key_noise, key_diag, key_scale = jax.random.split(base, 3)
    noise = jax.random.normal(key_noise, (SX, SY, LM, LM), jnp.float32)
    noise = (noise + jnp.swapaxes(noise, 2, 3)) / jnp.sqrt(2.0 * LM)
    diagonal = jax.random.uniform(key_diag, (SX, SY, LM), jnp.float32, 2.5, 4.0)
    scales = jnp.exp(jax.random.uniform(key_scale, (SX, SY, LM), jnp.float32, jnp.log(0.5), jnp.log(2.0)))
    matrix = noise + diagonal[..., None] * jnp.eye(LM, dtype=jnp.float32)
    return scales[..., :, None] * scales[..., None, :] * matrix


def draw_loads(key, part):
    base = jax.random.fold_in(key, 57)
    position = (jnp.arange(SX)[:, None] * SY + jnp.arange(SY)[None, :]).astype(jnp.float32) / (SX * SY - 1)
    values = jax.random.truncated_normal(base, -4.0, 4.0, (SX, SY, 2, LF, NCASE), jnp.float32)
    ramp = jnp.power(3.0, position)
    return values * ramp[:, :, None, None, None]


def level_of(stream_key, dims, pieces, least, largest):
    def one(dim, parts):
        steps = jax.random.uniform(jax.random.fold_in(jax.random.fold_in(stream_key, 6), dim), (parts,), jnp.float32, least / len(pieces), largest / len(pieces))
        return jnp.repeat(jnp.exp(steps), dims[dim] // parts).reshape((-1,) + (1,) * (len(dims) - dim - 1))

    factor_of = one(*pieces[0])
    for cut in pieces[1:]:
        factor_of = factor_of * one(*cut)
    return factor_of


def scatter_about(own_key, dims, deviation, bound, cuts=(), kind=jnp.bfloat16):
    drawn = jax.random.normal(own_key, dims, jnp.float32) * deviation
    if len(cuts) > 0:
        drawn = level_of(own_key, dims, cuts, -0.22, 0.18) * drawn
    return jnp.clip(drawn, min=-bound, max=bound).astype(kind)


def setup_inputs(seed: int = 0) -> dict:
    arg_keys = jax.random.split(jax.random.key(seed), 8)
    dual_ops = draw_dual_ops(jax.random.fold_in(arg_keys[7], 71), 0)
    loads = draw_loads(jax.random.fold_in(arg_keys[7], 71), 0)
    coarse_rhs = scatter_about(arg_keys[2], (SX, SY, 6, NCASE), (LF // 8), 288.0, ((0, 8), (1, 4)), jnp.float32)
    coarse_modes = draw_coarse_modes(jax.random.fold_in(arg_keys[7], 71), 0)
    free_mask = draw_free_mask(jax.random.fold_in(arg_keys[7], 71), 0)
    face_match = jax.vmap(lambda own: jax.random.permutation(own, LF))(jax.random.split(arg_keys[5], SX * SY * 2)).reshape((SX, SY, 2, LF)).astype(jnp.int32)
    coarse_rows = draw_coarse_rows(jax.random.fold_in(arg_keys[7], 71), 0)
    return dict(dual_ops=dual_ops, loads=loads, coarse_rhs=coarse_rhs, coarse_modes=coarse_modes, free_mask=free_mask, face_match=face_match, coarse_rows=coarse_rows)


HIGHEST = lax.Precision.HIGHEST

def lower_shift(values, dimension):
    widths = [(0, 0)] * values.ndim
    widths[dimension] = (1, 0)
    return lax.slice_in_dim(jnp.pad(values, widths), 0, values.shape[dimension], axis=dimension)

def upper_shift(values, dimension):
    widths = [(0, 0)] * values.ndim
    widths[dimension] = (0, 1)
    return lax.slice_in_dim(jnp.pad(values, widths), 1, values.shape[dimension] + 1, axis=dimension)

def pick_rows(values, indices):
    full_index = jnp.broadcast_to(indices[..., None], values.shape)
    return jnp.take_along_axis(values, full_index, axis=2)

def apply_dual(dual_ops, face_match, free_slots, field):
    face_slots = field.shape[3]
    case_count = field.shape[4]
    from_west = lower_shift(field[:, :, 0], 1)
    from_north = lower_shift(field[:, :, 1], 0)
    west_side = -pick_rows(from_west, face_match[:, :, 0])
    north_side = -pick_rows(from_north, face_match[:, :, 1])
    stacked = jnp.concatenate([field[:, :, 0], field[:, :, 1], west_side, north_side], axis=2)
    product = jnp.einsum('abij,abjc->abic', dual_ops, stacked, precision=HIGHEST)
    product = product.reshape(product.shape[0], product.shape[1], 4, face_slots, case_count)
    inverse = jnp.argsort(face_match, axis=-1).astype(jnp.int32)
    back_west = upper_shift(pick_rows(product[:, :, 2], inverse[:, :, 0]), 1)
    back_north = upper_shift(pick_rows(product[:, :, 3], inverse[:, :, 1]), 0)
    return (product[:, :, :2] - jnp.stack([back_west, back_north], axis=2)) * free_slots

def coarse_terms(coarse_modes, field):
    own_terms = jnp.einsum('abfjk,abfkc->abjc', coarse_modes[:, :, :, 0], field, precision=HIGHEST)
    east_terms = jnp.einsum('abjk,abkc->abjc', coarse_modes[:, :, 0, 1], field[:, :, 0], precision=HIGHEST)
    south_terms = jnp.einsum('abjk,abkc->abjc', coarse_modes[:, :, 1, 1], field[:, :, 1], precision=HIGHEST)
    return (own_terms, east_terms, south_terms)

def coarse_solve(coarse_rows, own_terms, east_terms, south_terms):
    summed = own_terms + lower_shift(east_terms, 1) + lower_shift(south_terms, 0)
    flat = summed.reshape(-1, summed.shape[-1])
    return jnp.einsum('abrjn,nc->abrjc', coarse_rows, flat, precision=HIGHEST)

def mode_images(coarse_modes, free_slots, alpha):
    east_face = jnp.einsum('abjk,abjc->abkc', coarse_modes[:, :, 0, 0], alpha[:, :, 0], precision=HIGHEST)
    east_face = east_face + jnp.einsum('abjk,abjc->abkc', coarse_modes[:, :, 0, 1], alpha[:, :, 1], precision=HIGHEST)
    south_face = jnp.einsum('abjk,abjc->abkc', coarse_modes[:, :, 1, 0], alpha[:, :, 0], precision=HIGHEST)
    south_face = south_face + jnp.einsum('abjk,abjc->abkc', coarse_modes[:, :, 1, 1], alpha[:, :, 2], precision=HIGHEST)
    return jnp.stack([east_face, south_face], axis=2) * free_slots

def reference(dual_ops, loads, coarse_rhs, coarse_modes, free_mask, face_match, coarse_rows):
    free_slots = free_mask.astype(jnp.float32)[..., None]

    def project(field):
        own_terms, east_terms, south_terms = coarse_terms(coarse_modes, field)
        alpha = coarse_solve(coarse_rows, own_terms, east_terms, south_terms)
        return field - mode_images(coarse_modes, free_slots, alpha)
    zeros_rhs = jnp.zeros_like(coarse_rhs)
    multipliers = mode_images(coarse_modes, free_slots, coarse_solve(coarse_rows, coarse_rhs, zeros_rhs, zeros_rhs))
    gradient = apply_dual(dual_ops, face_match, free_slots, multipliers) - loads * free_slots
    projected = project(gradient)
    norm_now = jnp.sum(projected * projected, axis=(0, 1, 2, 3))
    direction = projected
    for step in range(ITERS):
        image = apply_dual(dual_ops, face_match, free_slots, direction)
        step_size = norm_now / jnp.sum(direction * image, axis=(0, 1, 2, 3))
        multipliers = multipliers + step_size * direction
        gradient = gradient + step_size * image
        projected = project(gradient)
        norm_next = jnp.sum(projected * projected, axis=(0, 1, 2, 3))
        if step + 1 < ITERS:
            direction = projected + norm_next / norm_now * direction
            norm_now = norm_next
    return (multipliers, projected)
```

```python
import functools

import jax
import jax.numpy as jnp
from jax import lax
from jax.experimental import pallas as pl
from jax.experimental.pallas import tpu as pltpu
from jax.sharding import PartitionSpec as P

ITERS = 3
F32 = jnp.float32
BF16 = jnp.bfloat16
MESH = pl.DeviceIdType.MESH
EAST, SOUTH, WEST, NORTH = 0, 1, 2, 3
OPPOSITE = (WEST, NORTH, EAST, SOUTH)
ROUNDS = ITERS + 2
APPLIES = ITERS + 1


def split(values):
    high = values.astype(BF16)
    low = (values - high.astype(F32)).astype(BF16)
    return high, low


def dot32(left, right):
    return jnp.dot(left, right, preferred_element_type=F32)


def kernel(
    nx, ny, a_hbm, loads_hbm, rhs_ref, modes_ref, free_ref, match_ref, rows_ref,
    mult_ref, proj_ref,
    a_stage, a_high, a_low, loads4, pack, nb_pack, inverse, terms, alphas, alpha_pair,
    gt8, g_high, g_low, fg_high, fg_low, free4, put, perm, perm_back, vsplit, u_split,
    outbox, inbox, p_f, d_f, q_f, fp_f, fq_f,
    a_sem, l_sem, face_send, face_recv, pk_send, pk_recv, ld_send, ld_recv,
    gy_send, gy_recv, gx_send, gx_recv, cy_send, cy_recv, cx_send, cx_recv,
):
    lf = free_ref.shape[1]
    nc = mult_ref.shape[1]
    lm = a_high.shape[0]
    ncoarse = rows_ref.shape[2]
    wide = inverse.shape[3]
    me_x = lax.axis_index("gx")
    me_y = lax.axis_index("gy")
    exists = (me_y < ny - 1, me_x < nx - 1, me_y > 0, me_x > 0)
    place = ((me_x, me_y + 1), (me_x + 1, me_y), (me_x, me_y - 1), (me_x - 1, me_y))

    def face(f):
        return pl.ds(f * lf, lf)

    chunk = lm // 6
    a_copies = [
        pltpu.make_async_copy(
            a_hbm.at[pl.ds(i * chunk, chunk)], a_stage.at[pl.ds(i * chunk, chunk)], a_sem.at[i]
        )
        for i in range(6)
    ]
    for copy in a_copies:
        copy.start()
    l_copy = pltpu.make_async_copy(loads_hbm, loads4.at[pl.ds(0, 2 * lf)], l_sem)
    l_copy.start()

    barrier = pltpu.get_barrier_semaphore()
    for t in range(1, nx):
        pl.semaphore_signal(
            barrier, inc=1, device_id=(lax.rem(me_x + t, nx), me_y), device_id_type=MESH
        )
    for t in range(1, ny):
        pl.semaphore_signal(
            barrier, inc=1, device_id=(me_x, lax.rem(me_y + t, ny)), device_id_type=MESH
        )

    pack[...] = jnp.zeros_like(pack)
    for f in range(2):
        pack[f, 0:6, :] = modes_ref[f, 0]
        pack[f, 8:14, :] = modes_ref[f, 1]
        pack[f, 16:17, :] = free_ref[f : f + 1, :].astype(F32)

    row = lax.broadcasted_iota(jnp.int32, (ncoarse, wide), 0)
    col = lax.broadcasted_iota(jnp.int32, (ncoarse, wide), 1)
    slot = jnp.bitwise_and(col, 7)
    spread = jnp.where((row == 6 * jnp.right_shift(col, 3) + slot) & (slot < 6), 1.0, 0.0)
    inverse[me_x, me_y] = jnp.zeros((8, wide), F32)
    inverse[me_x, me_y, 0:6, :] = jnp.dot(
        rows_ref[0], spread.astype(F32), precision=lax.Precision.HIGHEST,
        preferred_element_type=F32,
    )
    terms[0, me_x, me_y] = jnp.zeros((16, nc), F32)
    terms[0, me_x, me_y, 0:6, :] = rhs_ref[...]

    pl.semaphore_wait(barrier, nx + ny - 2)

    def remote(src, dst, send, recv, where):
        return pltpu.make_async_remote_copy(
            src_ref=src, dst_ref=dst, send_sem=send, recv_sem=recv,
            device_id=where, device_id_type=MESH,
        )

    def neighbour_copy(f, src, dst, send, recv):
        return remote(src, dst, send, recv, place[f])

    for f in range(2):
        @pl.when(exists[f])
        def _():
            neighbour_copy(f, pack.at[f], nb_pack.at[f], pk_send.at[f], pk_recv.at[f]).start()

    def spread_column(view, send, recv):
        copies = []
        for t in range(1, ny):
            copies.append(remote(
                view(me_x, me_y), view(me_x, me_y), send.at[t], recv.at[t],
                (me_x, lax.rem(me_y + t, ny)),
            ))
        return copies

    def spread_row(view, send, recv):
        copies = []
        for t in range(1, nx):
            copies.append(remote(
                view(me_x), view(me_x), send.at[t], recv.at[t],
                (lax.rem(me_x + t, nx), me_y),
            ))
        return copies

    pending = []

    def begin(copies):
        for copy in copies:
            copy.start()
        pending.extend(copies)

    def finish(copies):
        for copy in copies:
            copy.wait_recv()

    def terms_column(r, rows):
        return spread_column(
            lambda x, y: terms.at[r, x, y, pl.ds(0, rows)], gy_send.at[r], gy_recv.at[r]
        )

    def terms_row(r, rows):
        return spread_row(
            lambda x: terms.at[r, x, :, pl.ds(0, rows)], gx_send.at[r], gx_recv.at[r]
        )

    inv_col = spread_column(lambda x, y: inverse.at[x, y], cy_send, cy_recv)
    inv_row = spread_row(lambda x: inverse.at[x], cx_send, cx_recv)
    rhs_col = terms_column(0, 8)
    rhs_row = terms_row(0, 8)
    begin(rhs_col)
    begin(inv_col)
    for f in range(2):
        @pl.when(exists[f])
        def _():
            neighbour_copy(
                f, loads_hbm.at[face(f)], loads4.at[face(2 + f)], ld_send.at[f], ld_recv.at[f]
            ).start()

    for f in range(4):
        @pl.when(jnp.logical_not(exists[f]))
        def _():
            for r in range(APPLIES):
                inbox[r, f] = jnp.zeros((lf, nc), F32)
    for f in range(2):
        @pl.when(jnp.logical_not(exists[2 + f]))
        def _():
            nb_pack[f] = jnp.zeros((24, lf), F32)
            loads4[face(2 + f), :] = jnp.zeros((lf, nc), F32)

    slots = lax.broadcasted_iota(jnp.int32, (lf, lf), 0)
    for f in range(2):
        back = jnp.where(slots == match_ref[f : f + 1, :], 1.0, 0.0).astype(F32)
        perm_back[f] = back.astype(BF16)
        perm[f] = (-jnp.transpose(back)).astype(BF16)

    def cast_chunk(i):
        a_copies[i].wait()
        part = a_stage[pl.ds(i * chunk, chunk), :]
        high, low = split(part)
        a_high[pl.ds(i * chunk, chunk), :] = high
        a_low[pl.ds(i * chunk, chunk), :] = low

    for i in range(3):
        cast_chunk(i)

    finish(rhs_col)
    begin(rhs_row)
    finish(inv_col)
    begin(inv_row)

    for i in range(3, 6):
        cast_chunk(i)

    for f in range(2):
        @pl.when(exists[2 + f])
        def _():
            neighbour_copy(f, pack.at[f], nb_pack.at[f], pk_send.at[f], pk_recv.at[f]).wait_recv()

    for f in range(4):
        put[...] = jnp.zeros_like(put)
        source = pack if f < 2 else nb_pack
        mask = source[f % 2, 16:17, :]
        owner = source[f % 2, 0:8, :] * mask
        other = source[f % 2, 8:16, :] * mask
        own_part, far_part = (owner, other) if f < 2 else (other, owner)
        put[0:8, :] = own_part
        put[8 * (f + 1) : 8 * (f + 2), :] = far_part
        high, low = split(own_part)
        gt8[0:8, face(f)] = high.astype(F32)
        gt8[8:16, face(f)] = low.astype(F32)
        q_f[face(f), :] = jnp.transpose(put[...])
        free4[face(f), :] = jnp.transpose(jnp.broadcast_to(mask, (nc, lf)))
    high, low = split(q_f[...])
    g_high[...] = high
    g_low[...] = low

    def split_field(ref):
        high, low = split(ref[...])
        vsplit[:, 0:nc] = high
        vsplit[:, nc : 2 * nc] = low

    def coarse_terms(r):
        both = dot32(gt8[...].astype(BF16), vsplit[...])
        terms[r, me_x, me_y, 0:8, :] = (
            both[0:8, 0:nc] + both[0:8, nc : 2 * nc] + both[8:16, 0:nc]
        )
        terms[r, me_x, me_y, 8:16, :] = jnp.zeros((8, nc), F32)

    def face_copy(r, f):
        g = OPPOSITE[f]
        return neighbour_copy(
            f, outbox.at[r, f], inbox.at[r, g], face_send.at[r, f], face_recv.at[r, g]
        )

    def apply_start(r, between):
        u_split[face(EAST), :] = vsplit[face(EAST), :]
        u_split[face(SOUTH), :] = vsplit[face(SOUTH), :]
        for f in range(2):
            u_split[face(2 + f), :] = dot32(perm[f], vsplit[face(2 + f), :]).astype(BF16)
        for f in (WEST, EAST, NORTH, SOUTH):
            both = dot32(a_high[face(f), :], u_split[...])
            z = dot32(a_low[face(f), :], u_split[:, 0:nc])
            z = z + both[:, 0:nc] + both[:, nc : 2 * nc]
            if f >= 2:
                high, low = split(z)
                z = dot32(perm_back[f - 2], high) + dot32(perm_back[f - 2], low)
            outbox[r, f] = z

            @pl.when(exists[f])
            def _():
                face_copy(r, f).start()

            if f == EAST:
                between()

    def face_arrived(r, f):
        g = OPPOSITE[f]

        @pl.when(exists[f])
        def _():
            remote(
                outbox.at[r, g], inbox.at[r, f], face_send.at[r, g], face_recv.at[r, f], place[f]
            ).wait_recv()

    def apply_finish(r, out):
        for f in (EAST, WEST, SOUTH, NORTH):
            face_arrived(r, f)
            delta = outbox[r, f] - inbox[r, f] if f < 2 else inbox[r, f] - outbox[r, f]
            out[face(f), :] = delta * free4[face(f), :]

    def solve(r):
        c = terms[r, :, :, 0:8, :].reshape(nx * ny * 8, nc)
        full = inverse[...].reshape(nx * ny * 8, wide)
        alpha = jnp.dot(
            full, c, precision=lax.Precision.HIGHEST, preferred_element_type=F32
        )
        alphas[...] = alpha.reshape(nx * ny, 8, nc)
        fill(0, me_x, me_y)
        for f in range(4):
            fill(f + 1, *place[f])
        return jnp.sum(c * alpha, axis=0, keepdims=True)

    def fill(which, x, y):
        for k, (dx, dy) in enumerate(((0, 0), (0, 1), (1, 0), (0, -1), (-1, 0))):
            xx = jnp.clip(x + dx, 0, nx - 1)
            yy = jnp.clip(y + dy, 0, ny - 1)
            high, low = split(alphas[xx * ny + yy])
            alpha_pair[which, 8 * k : 8 * k + 8, 0:nc] = high.astype(F32)
            alpha_pair[which, 8 * k : 8 * k + 8, nc : 2 * nc] = low.astype(F32)

    def product(left_high, left_low, right):
        both = dot32(left_high, right)
        return dot32(left_low, right[:, 0:nc]) + both[:, 0:nc] + both[:, nc : 2 * nc]

    def mode_image(f):
        return product(
            g_high[face(f), :], g_low[face(f), :], alpha_pair[0].astype(BF16)
        )

    def dual_mode_image(f):
        right = jnp.concatenate([alpha_pair[0], alpha_pair[f + 1]], axis=0).astype(BF16)
        return product(fg_high[face(f), :], fg_low[face(f), :], right)

    def own_sum(left, right):
        return jnp.sum(
            left[0 : 2 * lf, :] * right[0 : 2 * lf, :], axis=0, keepdims=True
        )

    def totals(r, rows):
        return jnp.sum(terms[r, :, :, 0:rows, :].reshape(nx * ny, rows, nc), axis=0)

    alpha_pair[...] = jnp.zeros_like(alpha_pair)

    vsplit[:, 0:nc] = g_high[...]
    vsplit[:, nc : 2 * nc] = g_low[...]
    apply_start(0, lambda: None)
    finish(rhs_row)
    finish(inv_row)
    solve(0)
    for f in range(2):
        mult_ref[face(f), :] = mode_image(f)
    for f in (EAST, WEST, SOUTH, NORTH):
        face_arrived(0, f)
        sign = 1.0 if f < 2 else -1.0
        mask = free4[face(f), :] * sign
        for half, values in enumerate((outbox[0, f] * mask, -inbox[0, f] * mask)):
            high, low = split(values)
            fg_high[face(f), half * nc : (half + 1) * nc] = high
            fg_low[face(f), half * nc : (half + 1) * nc] = low

    l_copy.wait()
    for f in range(2):
        @pl.when(exists[2 + f])
        def _():
            neighbour_copy(
                f, loads_hbm.at[face(f)], loads4.at[face(2 + f)], ld_send.at[f], ld_recv.at[f]
            ).wait_recv()
    for f in range(4):
        p_f[face(f), :] = dual_mode_image(f) - loads4[face(f), :] * free4[face(f), :]

    def round_trip(r, rows, apply, out):
        column = terms_column(r, rows)
        line = terms_row(r, rows)
        begin(column)

        def relay():
            finish(column)
            begin(line)

        if apply:
            apply_start(r, relay)
            finish(line)
        else:
            relay()
            finish(line)
        inner = solve(r)
        if apply:
            apply_finish(r, out)
        return inner

    split_field(p_f)
    coarse_terms(1)
    round_trip(1, 8, True, q_f)
    for f in range(4):
        p = p_f[face(f), :] - mode_image(f)
        p_f[face(f), :] = p
        d_f[face(f), :] = p
        q = q_f[face(f), :] - dual_mode_image(f)
        q_f[face(f), :] = q
        fp_f[face(f), :] = q

    norm = None
    for step in range(ITERS):
        r = step + 2
        last = step + 1 == ITERS
        split_field(q_f)
        coarse_terms(r)
        rows = 8 if last else 16
        terms[r, me_x, me_y, 6:7, :] = own_sum(d_f, q_f)
        if not last:
            terms[r, me_x, me_y, 7:8, :] = own_sum(p_f, p_f if step == 0 else q_f)
            terms[r, me_x, me_y, 8:9, :] = own_sum(q_f, q_f)
        inner = round_trip(r, rows, not last, fq_f)
        total = totals(r, rows)
        curvature = total[6:7, :]
        if step == 0:
            norm = total[7:8, :]
            cross = curvature
        else:
            cross = total[7:8, :]
        size = norm / curvature
        mult_ref[...] = mult_ref[...] + size * d_f[0 : 2 * lf, :]
        if last:
            for f in range(2):
                proj_ref[face(f), :] = p_f[face(f), :] + size * (q_f[face(f), :] - mode_image(f))
            break
        norm_next = norm + 2.0 * size * cross + size * size * (total[8:9, :] - inner)
        ratio = norm_next / norm
        for f in range(4):
            q = q_f[face(f), :]
            p = p_f[face(f), :] + size * (q - mode_image(f))
            p_f[face(f), :] = p
            fp = fp_f[face(f), :] + size * (fq_f[face(f), :] - dual_mode_image(f))
            fp_f[face(f), :] = fp
            d_f[face(f), :] = p + ratio * d_f[face(f), :]
            q_f[face(f), :] = fp + ratio * q
        norm = norm_next

    for copy in pending:
        copy.wait_send()
    for f in range(2):
        @pl.when(exists[f])
        def _():
            neighbour_copy(f, pack.at[f], nb_pack.at[f], pk_send.at[f], pk_recv.at[f]).wait_send()
            neighbour_copy(
                f, loads_hbm.at[face(f)], loads4.at[face(2 + f)], ld_send.at[f], ld_recv.at[f]
            ).wait_send()
    for f in range(4):
        @pl.when(exists[f])
        def _():
            for r in range(APPLIES):
                face_copy(r, f).wait_send()


def solution(mesh):
    nx, ny = mesh.shape["gx"], mesh.shape["gy"]

    def local(dual_ops, loads, coarse_rhs, coarse_modes, free_mask, face_match, coarse_rows):
        lm = dual_ops.shape[-1]
        lf, nc = loads.shape[-2:]
        wide = nx * ny * 8
        vmem = pl.BlockSpec(memory_space=pltpu.VMEM)
        hbm = pl.BlockSpec(memory_space=pl.ANY)
        dma = pltpu.SemaphoreType.DMA
        out = jax.ShapeDtypeStruct((2 * lf, nc), F32)
        field = pltpu.VMEM((lm, nc), F32)
        mult, proj = pl.pallas_call(
            functools.partial(kernel, nx, ny),
            out_shape=(out, out),
            in_specs=[hbm, hbm] + [vmem] * 5,
            out_specs=(vmem, vmem),
            scratch_shapes=[
                pltpu.VMEM((lm, lm), F32),
                pltpu.VMEM((lm, lm), BF16),
                pltpu.VMEM((lm, lm), BF16),
                field,
                pltpu.VMEM((2, 24, lf), F32),
                pltpu.VMEM((2, 24, lf), F32),
                pltpu.VMEM((nx, ny, 8, wide), F32),
                pltpu.VMEM((ROUNDS, nx, ny, 16, nc), F32),
                pltpu.VMEM((nx * ny, 8, nc), F32),
                pltpu.VMEM((5, nc, 2 * nc), F32),
                pltpu.VMEM((16, lm), F32),
                pltpu.VMEM((lm, nc), BF16),
                pltpu.VMEM((lm, nc), BF16),
                pltpu.VMEM((lm, 2 * nc), BF16),
                pltpu.VMEM((lm, 2 * nc), BF16),
                field,
                pltpu.VMEM((nc, lf), F32),
                pltpu.VMEM((2, lf, lf), BF16),
                pltpu.VMEM((2, lf, lf), BF16),
                pltpu.VMEM((lm, 2 * nc), BF16),
                pltpu.VMEM((lm, 2 * nc), BF16),
                pltpu.VMEM((APPLIES, 4, lf, nc), F32),
                pltpu.VMEM((APPLIES, 4, lf, nc), F32),
                field, field, field, field, field,
                dma((6,)),
                dma,
                dma((APPLIES, 4)),
                dma((APPLIES, 4)),
                dma((2,)), dma((2,)), dma((2,)), dma((2,)),
                dma((ROUNDS, ny)), dma((ROUNDS, ny)),
                dma((ROUNDS, nx)), dma((ROUNDS, nx)),
                dma((ny,)), dma((ny,)), dma((nx,)), dma((nx,)),
            ],
            compiler_params=pltpu.CompilerParams(
                collective_id=0, has_side_effects=True, vmem_limit_bytes=58 * 1024 * 1024
            ),
        )(
            dual_ops.reshape(lm, lm),
            loads.reshape(2 * lf, nc),
            coarse_rhs.reshape(coarse_rhs.shape[2:]),
            coarse_modes.reshape(coarse_modes.shape[2:]),
            free_mask.reshape(free_mask.shape[2:]),
            face_match.reshape(face_match.shape[2:]),
            coarse_rows.reshape(coarse_rows.shape[2:]),
        )
        return (mult.reshape(1, 1, 2, lf, nc), proj.reshape(1, 1, 2, lf, nc))

    in_specs = (
        P("gx", "gy", None, None),
        P("gx", "gy", None, None, None),
        P("gx", "gy", None, None),
        P("gx", "gy", None, None, None, None),
        P("gx", "gy", None, None),
        P("gx", "gy", None, None),
        P("gx", "gy", None, None, None),
    )
    out_specs = (P("gx", "gy", None, None, None), P("gx", "gy", None, None, None))
    return jax.shard_map(local, mesh=mesh, in_specs=in_specs, out_specs=out_specs, check_vma=False)
```

```python
import functools

import jax
import jax.numpy as jnp
from jax import lax
from jax.experimental import pallas as pl
from jax.experimental.pallas import tpu as pltpu
from jax.sharding import PartitionSpec as P

ITERS = 3
F32 = jnp.float32
BF16 = jnp.bfloat16
MESH = pl.DeviceIdType.MESH
EAST, SOUTH, WEST, NORTH = 0, 1, 2, 3
OPPOSITE = (WEST, NORTH, EAST, SOUTH)
ROUNDS = ITERS + 2
APPLIES = ITERS + 1


def split(values):
    high = values.astype(BF16)
    low = (values - high.astype(F32)).astype(BF16)
    return high, low


def dot32(left, right):
    return jnp.dot(left, right, preferred_element_type=F32)


def kernel(
    nx, ny, a_hbm, loads_hbm, rhs_ref, modes_ref, free_ref, match_ref, rows_ref,
    mult_ref, proj_ref,
    a_stage, a_high, a_low, loads4, pack, nb_pack, own_rows, inverse, terms, alphas, alpha_pair,
    gt8, g_pair, fg_pair, free4, put, perm, perm_back, vsplit, u_split,
    outbox, inbox, p_f, d_f, q_f, fp_f, fq_f,
    a_sem, l_sem, face_send, face_recv, pk_send, pk_recv, ld_send, ld_recv,
    gy_send, gy_recv, gx_send, gx_recv, cy_send, cy_recv, cx_send, cx_recv,
):
    lf = free_ref.shape[1]
    nc = mult_ref.shape[1]
    lm = a_high.shape[0]
    ncoarse = rows_ref.shape[3]
    wide = inverse.shape[3]
    half = g_pair.shape[1] // 2
    me_x = lax.axis_index("gx")
    me_y = lax.axis_index("gy")
    exists = (me_y < ny - 1, me_x < nx - 1, me_y > 0, me_x > 0)
    place = ((me_x, me_y + 1), (me_x + 1, me_y), (me_x, me_y - 1), (me_x - 1, me_y))

    def face(f):
        return pl.ds(f * lf, lf)

    chunk = lm // 6
    a_copies = [
        pltpu.make_async_copy(
            a_hbm.at[pl.ds(i * chunk, chunk)], a_stage.at[pl.ds(i * chunk, chunk)], a_sem.at[i]
        )
        for i in range(6)
    ]
    for copy in a_copies:
        copy.start()
    l_copy = pltpu.make_async_copy(loads_hbm, loads4.at[pl.ds(0, 2 * lf)], l_sem)
    l_copy.start()

    barrier = pltpu.get_barrier_semaphore()
    for t in range(1, nx):
        pl.semaphore_signal(
            barrier, inc=1, device_id=(lax.rem(me_x + t, nx), me_y), device_id_type=MESH
        )
    for t in range(1, ny):
        pl.semaphore_signal(
            barrier, inc=1, device_id=(me_x, lax.rem(me_y + t, ny)), device_id_type=MESH
        )

    pack[...] = jnp.zeros_like(pack)
    for f in range(2):
        for m in range(6):
            pack[f, m : m + 1, :] = modes_ref[f, m, 0:1, :]
            pack[f, 8 + m : 9 + m, :] = modes_ref[f, m, 1:2, :]
        pack[f, 16:17, :] = free_ref[f : f + 1, :].astype(F32)

    row = lax.broadcasted_iota(jnp.int32, (ncoarse, wide), 0)
    col = lax.broadcasted_iota(jnp.int32, (ncoarse, wide), 1)
    slot = jnp.bitwise_and(col, 7)
    spread = jnp.where((row == 6 * jnp.right_shift(col, 3) + slot) & (slot < 6), 1.0, 0.0)
    own_rows[...] = jnp.zeros_like(own_rows)
    for m in range(6):
        own_rows[m : m + 1, :] = rows_ref[0, m]
    inverse[me_x, me_y] = jnp.dot(
        own_rows[...], spread.astype(F32), precision=lax.Precision.HIGHEST,
        preferred_element_type=F32,
    )
    terms[0, me_x, me_y] = jnp.zeros((16, nc), F32)
    for m in range(6):
        terms[0, me_x, me_y, m : m + 1, :] = rhs_ref[m]

    pl.semaphore_wait(barrier, nx + ny - 2)

    def remote(src, dst, send, recv, where):
        return pltpu.make_async_remote_copy(
            src_ref=src, dst_ref=dst, send_sem=send, recv_sem=recv,
            device_id=where, device_id_type=MESH,
        )

    def neighbour_copy(f, src, dst, send, recv):
        return remote(src, dst, send, recv, place[f])

    for f in range(2):
        @pl.when(exists[f])
        def _():
            neighbour_copy(f, pack.at[f], nb_pack.at[f], pk_send.at[f], pk_recv.at[f]).start()

    def spread_column(view, send, recv):
        copies = []
        for t in range(1, ny):
            copies.append(remote(
                view(me_x, me_y), view(me_x, me_y), send.at[t], recv.at[t],
                (me_x, lax.rem(me_y + t, ny)),
            ))
        return copies

    def spread_row(view, send, recv):
        copies = []
        for t in range(1, nx):
            copies.append(remote(
                view(me_x), view(me_x), send.at[t], recv.at[t],
                (lax.rem(me_x + t, nx), me_y),
            ))
        return copies

    pending = []

    def begin(copies):
        for copy in copies:
            copy.start()
        pending.extend(copies)

    def finish(copies):
        for copy in copies:
            copy.wait_recv()

    def terms_column(r, rows):
        return spread_column(
            lambda x, y: terms.at[r, x, y, pl.ds(0, rows)], gy_send.at[r], gy_recv.at[r]
        )

    def terms_row(r, rows):
        return spread_row(
            lambda x: terms.at[r, x, :, pl.ds(0, rows)], gx_send.at[r], gx_recv.at[r]
        )

    inv_col = spread_column(lambda x, y: inverse.at[x, y], cy_send, cy_recv)
    inv_row = spread_row(lambda x: inverse.at[x], cx_send, cx_recv)
    rhs_col = terms_column(0, 8)
    rhs_row = terms_row(0, 8)
    begin(rhs_col)
    begin(inv_col)
    for f in range(2):
        @pl.when(exists[f])
        def _():
            neighbour_copy(
                f, loads_hbm.at[face(f)], loads4.at[face(2 + f)], ld_send.at[f], ld_recv.at[f]
            ).start()

    for f in range(4):
        @pl.when(jnp.logical_not(exists[f]))
        def _():
            for r in range(APPLIES):
                inbox[r, f] = jnp.zeros((lf, nc), F32)
    for f in range(2):
        @pl.when(jnp.logical_not(exists[2 + f]))
        def _():
            nb_pack[f] = jnp.zeros((24, lf), F32)
            loads4[face(2 + f), :] = jnp.zeros((lf, nc), F32)

    slots = lax.broadcasted_iota(jnp.int32, (lf, lf), 0)
    for f in range(2):
        back = jnp.where(slots == match_ref[f : f + 1, :], 1.0, 0.0).astype(F32)
        perm_back[f] = back.astype(BF16)
        perm[f] = (-jnp.transpose(back)).astype(BF16)

    def cast_chunk(i):
        a_copies[i].wait()
        part = a_stage[pl.ds(i * chunk, chunk), :]
        high, low = split(part)
        a_high[pl.ds(i * chunk, chunk), :] = high
        a_low[pl.ds(i * chunk, chunk), :] = low

    for i in range(3):
        cast_chunk(i)

    finish(rhs_col)
    begin(rhs_row)
    finish(inv_col)
    begin(inv_row)

    for i in range(3, 6):
        cast_chunk(i)

    for f in range(2):
        @pl.when(exists[2 + f])
        def _():
            neighbour_copy(f, pack.at[f], nb_pack.at[f], pk_send.at[f], pk_recv.at[f]).wait_recv()

    for f in range(4):
        put[...] = jnp.zeros_like(put)
        source = pack if f < 2 else nb_pack
        mask = source[f % 2, 16:17, :]
        owner = source[f % 2, 0:8, :] * mask
        other = source[f % 2, 8:16, :] * mask
        own_part, far_part = (owner, other) if f < 2 else (other, owner)
        put[0:8, :] = own_part
        put[8 * (f + 1) : 8 * (f + 2), :] = far_part
        high, low = split(own_part)
        gt8[0:8, face(f)] = high.astype(F32)
        gt8[8:16, face(f)] = low.astype(F32)
        q_f[face(f), :] = jnp.transpose(put[...])
        free4[face(f), :] = jnp.transpose(jnp.broadcast_to(mask, (nc, lf)))
    high, low = split(q_f[...])
    vsplit[:, 0:nc] = high
    vsplit[:, nc : 2 * nc] = low
    g_pair[...] = jnp.concatenate([high[:, 0:half], low[:, 0:half]], axis=1)

    def split_field(ref):
        high, low = split(ref[...])
        vsplit[:, 0:nc] = high
        vsplit[:, nc : 2 * nc] = low

    def coarse_terms(r):
        both = dot32(gt8[...].astype(BF16), vsplit[...])
        terms[r, me_x, me_y, 0:8, :] = (
            both[0:8, 0:nc] + both[0:8, nc : 2 * nc] + both[8:16, 0:nc]
        )
        terms[r, me_x, me_y, 8:16, :] = jnp.zeros((8, nc), F32)

    def face_copy(r, f):
        g = OPPOSITE[f]
        return neighbour_copy(
            f, outbox.at[r, f], inbox.at[r, g], face_send.at[r, f], face_recv.at[r, g]
        )

    def apply_start(r, between):
        u_split[face(EAST), :] = vsplit[face(EAST), :]
        u_split[face(SOUTH), :] = vsplit[face(SOUTH), :]
        for f in range(2):
            u_split[face(2 + f), :] = dot32(perm[f], vsplit[face(2 + f), :]).astype(BF16)
        for f in (WEST, EAST, NORTH, SOUTH):
            both = dot32(a_high[face(f), :], u_split[...])
            z = dot32(a_low[face(f), :], u_split[:, 0:nc])
            z = z + both[:, 0:nc] + both[:, nc : 2 * nc]
            if f >= 2:
                high, low = split(z)
                moved = dot32(perm_back[f - 2], jnp.concatenate([high, low], axis=1))
                z = moved[:, 0:nc] + moved[:, nc : 2 * nc]
            outbox[r, f] = z

            @pl.when(exists[f])
            def _():
                face_copy(r, f).start()

            if f == EAST:
                between()

    def face_arrived(r, f):
        g = OPPOSITE[f]

        @pl.when(exists[f])
        def _():
            remote(
                outbox.at[r, g], inbox.at[r, f], face_send.at[r, g], face_recv.at[r, f], place[f]
            ).wait_recv()

    def apply_finish(r, out):
        for f in (EAST, WEST, SOUTH, NORTH):
            face_arrived(r, f)
            delta = outbox[r, f] - inbox[r, f] if f < 2 else inbox[r, f] - outbox[r, f]
            out[face(f), :] = delta * free4[face(f), :]

    def solve(r):
        c = terms[r, :, :, 0:8, :].reshape(nx * ny * 8, nc)
        full = inverse[...].reshape(nx * ny * 8, wide)
        alpha = jnp.dot(
            full, c, precision=lax.Precision.HIGHEST, preferred_element_type=F32
        )
        alphas[...] = alpha.reshape(nx * ny, 8, nc)
        fill(0, me_x, me_y)
        for f in range(4):
            fill(f + 1, *place[f])
        return jnp.sum(c * alpha, axis=0, keepdims=True)

    def fill(which, x, y):
        for k, (dx, dy) in enumerate(((0, 0), (0, 1), (1, 0), (0, -1), (-1, 0))):
            xx = jnp.clip(x + dx, 0, nx - 1)
            yy = jnp.clip(y + dy, 0, ny - 1)
            high, low = split(alphas[xx * ny + yy])
            alpha_pair[which, 8 * k : 8 * k + 8, 0:nc] = high.astype(F32)
            alpha_pair[which, 8 * k : 8 * k + 8, nc : 2 * nc] = low.astype(F32)
            alpha_pair[which, half + 8 * k : half + 8 * k + 8, 0:nc] = high.astype(F32)

    def mode_image(f):
        right = alpha_pair[0].astype(BF16)
        both = dot32(g_pair[face(f), :], right)
        return both[:, 0:nc] + both[:, nc : 2 * nc]

    def dual_mode_image(f):
        own, far = alpha_pair[0], alpha_pair[f + 1]
        right = jnp.concatenate(
            [own[0:half], far[0:half], own[half:], far[half:]], axis=0
        ).astype(BF16)
        both = dot32(fg_pair[face(f), :], right)
        return both[:, 0:nc] + both[:, nc : 2 * nc]

    def own_sum(left, right):
        return jnp.sum(
            left[0 : 2 * lf, :] * right[0 : 2 * lf, :], axis=0, keepdims=True
        )

    def totals(r, rows):
        return jnp.sum(terms[r, :, :, 0:rows, :].reshape(nx * ny, rows, nc), axis=0)

    alpha_pair[...] = jnp.zeros_like(alpha_pair)

    apply_start(0, lambda: None)
    finish(rhs_row)
    finish(inv_row)
    solve(0)
    for f in range(2):
        mult_ref[face(f), :] = mode_image(f)
    for f in (EAST, WEST, SOUTH, NORTH):
        face_arrived(0, f)
        sign = 1.0 if f < 2 else -1.0
        mask = free4[face(f), :] * sign
        own_high, own_low = split(outbox[0, f] * mask)
        far_high, far_low = split(-inbox[0, f] * mask)
        fg_pair[face(f), :] = jnp.concatenate(
            [part[:, 0:half] for part in (own_high, far_high, own_low, far_low)], axis=1
        )

    l_copy.wait()
    for f in range(2):
        @pl.when(exists[2 + f])
        def _():
            neighbour_copy(
                f, loads_hbm.at[face(f)], loads4.at[face(2 + f)], ld_send.at[f], ld_recv.at[f]
            ).wait_recv()
    for f in range(4):
        p_f[face(f), :] = dual_mode_image(f) - loads4[face(f), :] * free4[face(f), :]

    def round_trip(r, rows, apply, out):
        column = terms_column(r, rows)
        line = terms_row(r, rows)
        begin(column)

        def relay():
            finish(column)
            begin(line)

        if apply:
            apply_start(r, relay)
            finish(line)
        else:
            relay()
            finish(line)
        inner = solve(r)
        if apply:
            apply_finish(r, out)
        return inner

    split_field(p_f)
    coarse_terms(1)
    round_trip(1, 8, True, q_f)
    for f in range(4):
        p = p_f[face(f), :] - mode_image(f)
        p_f[face(f), :] = p
        d_f[face(f), :] = p
        q = q_f[face(f), :] - dual_mode_image(f)
        q_f[face(f), :] = q
        fp_f[face(f), :] = q

    norm = None
    for step in range(ITERS):
        r = step + 2
        last = step + 1 == ITERS
        split_field(q_f)
        coarse_terms(r)
        rows = 8 if last else 16
        terms[r, me_x, me_y, 6:7, :] = own_sum(d_f, q_f)
        if not last:
            terms[r, me_x, me_y, 7:8, :] = own_sum(p_f, p_f if step == 0 else q_f)
            terms[r, me_x, me_y, 8:9, :] = own_sum(q_f, q_f)
        inner = round_trip(r, rows, not last, fq_f)
        total = totals(r, rows)
        curvature = total[6:7, :]
        if step == 0:
            norm = total[7:8, :]
            cross = curvature
        else:
            cross = total[7:8, :]
        size = norm / curvature
        mult_ref[...] = mult_ref[...] + size * d_f[0 : 2 * lf, :]
        if last:
            for f in range(2):
                proj_ref[face(f), :] = p_f[face(f), :] + size * (q_f[face(f), :] - mode_image(f))
            break
        norm_next = norm + 2.0 * size * cross + size * size * (total[8:9, :] - inner)
        ratio = norm_next / norm
        for f in range(4):
            q = q_f[face(f), :]
            p = p_f[face(f), :] + size * (q - mode_image(f))
            p_f[face(f), :] = p
            fp = fp_f[face(f), :] + size * (fq_f[face(f), :] - dual_mode_image(f))
            fp_f[face(f), :] = fp
            d_f[face(f), :] = p + ratio * d_f[face(f), :]
            q_f[face(f), :] = fp + ratio * q
        norm = norm_next

    for copy in pending:
        copy.wait_send()
    for f in range(2):
        @pl.when(exists[f])
        def _():
            neighbour_copy(f, pack.at[f], nb_pack.at[f], pk_send.at[f], pk_recv.at[f]).wait_send()
            neighbour_copy(
                f, loads_hbm.at[face(f)], loads4.at[face(2 + f)], ld_send.at[f], ld_recv.at[f]
            ).wait_send()
    for f in range(4):
        @pl.when(exists[f])
        def _():
            for r in range(APPLIES):
                face_copy(r, f).wait_send()


def hand_over(mult_in, proj_in, mult_out, proj_out, sem):
    copies = [
        pltpu.make_async_copy(mult_in, mult_out, sem.at[0]),
        pltpu.make_async_copy(proj_in, proj_out, sem.at[1]),
    ]
    for copy in copies:
        copy.start()
    for copy in copies:
        copy.wait()


def solution(mesh):
    nx, ny = mesh.shape["gx"], mesh.shape["gy"]

    def local(dual_ops, loads, coarse_rhs, coarse_modes, free_mask, face_match, coarse_rows):
        lm = dual_ops.shape[-1]
        lf, nc = loads.shape[-2:]
        wide = nx * ny * 8
        half = 64
        vmem = pl.BlockSpec(memory_space=pltpu.VMEM)
        hbm = pl.BlockSpec(memory_space=pl.ANY)
        dma = pltpu.SemaphoreType.DMA
        out = jax.ShapeDtypeStruct((2 * lf, nc), F32)
        field = pltpu.VMEM((lm, nc), F32)
        mult, proj = pl.pallas_call(
            functools.partial(kernel, nx, ny),
            out_shape=(out, out),
            in_specs=[hbm, hbm] + [vmem] * 5,
            out_specs=(vmem, vmem),
            scratch_shapes=[
                pltpu.VMEM((lm, lm), F32),
                pltpu.VMEM((lm, lm), BF16),
                pltpu.VMEM((lm, lm), BF16),
                field,
                pltpu.VMEM((2, 24, lf), F32),
                pltpu.VMEM((2, 24, lf), F32),
                pltpu.VMEM((8, nx * ny * 6), F32),
                pltpu.VMEM((nx, ny, 8, wide), F32),
                pltpu.VMEM((ROUNDS, nx, ny, 16, nc), F32),
                pltpu.VMEM((nx * ny, 8, nc), F32),
                pltpu.VMEM((5, 2 * half, 2 * nc), F32),
                pltpu.VMEM((16, lm), F32),
                pltpu.VMEM((lm, 2 * half), BF16),
                pltpu.VMEM((lm, 4 * half), BF16),
                field,
                pltpu.VMEM((nc, lf), F32),
                pltpu.VMEM((2, lf, lf), BF16),
                pltpu.VMEM((2, lf, lf), BF16),
                pltpu.VMEM((lm, 2 * nc), BF16),
                pltpu.VMEM((lm, 2 * nc), BF16),
                pltpu.VMEM((APPLIES, 4, lf, nc), F32),
                pltpu.VMEM((APPLIES, 4, lf, nc), F32),
                field, field, field, field, field,
                dma((6,)),
                dma,
                dma((APPLIES, 4)),
                dma((APPLIES, 4)),
                dma((2,)), dma((2,)), dma((2,)), dma((2,)),
                dma((ROUNDS, ny)), dma((ROUNDS, ny)),
                dma((ROUNDS, nx)), dma((ROUNDS, nx)),
                dma((ny,)), dma((ny,)), dma((nx,)), dma((nx,)),
            ],
            compiler_params=pltpu.CompilerParams(
                collective_id=0, has_side_effects=True, vmem_limit_bytes=58 * 1024 * 1024
            ),
        )(
            dual_ops.reshape(lm, lm),
            loads.reshape(2 * lf, nc),
            jnp.swapaxes(coarse_rhs[0], 0, 1),
            jnp.swapaxes(coarse_modes[0, 0], 1, 2),
            free_mask.reshape(free_mask.shape[2:]),
            face_match.reshape(face_match.shape[2:]),
            coarse_rows[0, 0][:, :, None, :],
        )
        mult, proj = pl.pallas_call(
            hand_over,
            out_shape=(out, out),
            in_specs=[hbm, hbm],
            out_specs=(hbm, hbm),
            scratch_shapes=[dma((2,))],
        )(mult, proj)
        return (mult.reshape(1, 1, 2, lf, nc), proj.reshape(1, 1, 2, lf, nc))

    in_specs = (
        P("gx", "gy", None, None),
        P("gx", "gy", None, None, None),
        P("gx", "gy", None, None),
        P("gx", "gy", None, None, None, None),
        P("gx", "gy", None, None),
        P("gx", "gy", None, None),
        P("gx", "gy", None, None, None),
    )
    out_specs = (P("gx", "gy", None, None, None), P("gx", "gy", None, None, None))
    return jax.shard_map(local, mesh=mesh, in_specs=in_specs, out_specs=out_specs, check_vma=False)
```
